32 devices in a mesh: tgt: 8 (over z, x), src: 4 (over y, core).
Axes of the slice: x: 2, y: 2, z: 4, core: 2. Of those that a mesh axis runs over, the one named last changes fastest.
Arguments:
- kernel: bfloat16 [8, 8192, 8192], P(None, 'tgt', 'src'), may hold values from -0.0234375 to 0.0234375
- history: bfloat16 [8, 128, 8192], P(None, None, 'src'), may hold values from -1 to 1
- driving: float32 [128, 8192], P(None, ('tgt', 'src')), may hold values from -6 to 6
- load_rate: float32 [8192], P(('tgt', 'src')), may hold values from -0.3 to 0.3
- rate_gain: float32 [8192], P(('tgt', 'src')), may hold values from 0.3 to 1.2
- friction: float32 [8192], P(('tgt', 'src')), may hold values from 0.2 to 1
- state_decay: float32 [8192], P(('tgt', 'src')), may hold values from 0.3 to 0.95
Outputs:
- stress: float32 [128, 8192], P(None, ('tgt', 'src'))
- state: float32 [128, 8192], P(None, ('tgt', 'src'))
- slip_rate: bfloat16 [128, 8192], P(None, ('tgt', 'src'))
The draws below stay inside these ranges and needn't reach their ends.
All inputs are finite; a program needn't handle non-finite values.
Results may differ from the reference program's by a relative error of at most 0.0032.
Values may be sent and summed in bfloat16 or wider, within the bound.
No kernel may reach another device: no remote copies, remote signals or barrier semaphores. Data moves between devices by JAX's collectives and lax.ppermute only.
A program may use at most 128 MiB of HBM per device.

```python
import math
import jax
import jax.numpy as jnp
from jax import lax

E = 8192
LAGS = 8
SCEN = 128
STEPS = 6


def level_of(own_key, extent, cuts, smallest, high):
    def one(position, blocks):
        heights = jax.random.uniform(jax.random.fold_in(jax.random.fold_in(own_key, 6), position), (blocks,), jnp.float32, smallest / len(cuts), high / len(cuts))
        return jnp.repeat(jnp.exp(heights), extent[position] // blocks).reshape((-1,) + (1,) * (len(extent) - position - 1))

    loudness = one(*cuts[0])
    for cut in cuts[1:]:
        loudness = loudness * one(*cut)
    return loudness


def normal_values(own_key, extent, spread, limit, split=(), kind=jnp.bfloat16):
    level = level_of(own_key, extent, split, -0.22, 0.18) if split else 1.0
    array = jax.random.normal(own_key, extent, jnp.float32) * spread * level
    return jnp.minimum(jnp.maximum(array, -limit), limit).astype(kind)


def setup_inputs(seed: int = 0) -> dict:
    seeds = jax.random.split(jax.random.key(seed), 8)
    kernel = normal_values(seeds[0], (LAGS, E, E), (LAGS * E) ** -0.5, 0.0234375, ((1, 8), (2, 4)))
    history = jnp.clip(jax.random.uniform(seeds[1], (LAGS, SCEN, E), jnp.float32, -1.0, 1.0) * level_of(seeds[1], (LAGS, SCEN, E), ((2, 4),), -0.4, 0.0), -1.0, 1.0).astype(jnp.bfloat16)
    driving = normal_values(seeds[2], (SCEN, E), 1.0, 6.0, ((1, 32),), jnp.float32)
    load_rate = jnp.clip(jax.random.uniform(seeds[3], (E,), jnp.float32, -0.3, 0.3) * level_of(seeds[3], (E,), ((0, 32),), -0.4, 0.0), -0.3, 0.3)
    rate_gain = jnp.clip(jnp.exp(math.log(1.2) - 1.3862944 * jax.random.uniform(seeds[4], (E,), jnp.float32) ** level_of(seeds[4], (E,), ((0, 32),), -0.2, 0.2)), 0.3, 1.2)
    friction = jnp.clip(0.2 + 0.8 * jax.random.uniform(seeds[5], (E,), jnp.float32) ** level_of(seeds[5], (E,), ((0, 32),), -0.2, 0.2), 0.2, 1.0)
    state_decay = jnp.clip(0.3 + 0.65 * jax.random.uniform(seeds[6], (E,), jnp.float32) ** level_of(seeds[6], (E,), ((0, 32),), -0.2, 0.2), 0.3, 0.95)
    return {"kernel": kernel, "history": history, "driving": driving, "load_rate": load_rate, "rate_gain": rate_gain, "friction": friction, "state_decay": state_decay}


def reference(kernel, history, driving, load_rate, rate_gain, friction, state_decay):
    state = jnp.zeros(driving.shape, jnp.float32)
    recent = history

    def add_lag(summed, operands):
        lag_kernel, lag_rates = operands
        term = lax.dot_general(lag_rates.astype(jnp.float32), lag_kernel.astype(jnp.float32),
                               (((1,), (1,)), ((), ())), precision=lax.Precision.HIGHEST)
        return summed + term, None

    stress = driving
    slip_rate = history[0]
    for section in range(STEPS):
        summed, _ = lax.scan(add_lag, jnp.zeros(driving.shape, jnp.float32), (kernel, recent))
        stress = driving + (section + 1) * load_rate[None, :] - summed
        slip_rate = jnp.tanh(rate_gain[None, :] * (stress - friction[None, :] * state)).astype(jnp.bfloat16)
        state = state_decay[None, :] * state + slip_rate.astype(jnp.float32)
        recent = jnp.concatenate([slip_rate[None], recent[:-1]], axis=0)
    return stress, state, slip_rate
```

```python
import jax
import jax.numpy as jnp
from jax import lax
from jax.sharding import PartitionSpec as P

STEPS = 6
AXES = ("tgt", "src")


def marching(n_tgt, n_src):
    fold = n_tgt // n_src
    places = [(q, x, s) for q in range(n_src) for x in range(fold) for s in range(n_src)]

    def flat(q, x, s):
        return (q * fold + x) * n_src + s

    def permute(value, move):
        pairs = [(flat(*place), flat(*move(*place))) for place in places]
        return lax.ppermute(value, AXES, pairs)

    def scatter_sum(pieces, s):
        bit = 1
        while len(pieces) > 1:
            upper = (s // bit) % 2 == 1
            keep = [jnp.where(upper, b, a) for a, b in zip(pieces[0::2], pieces[1::2])]
            send = [jnp.where(upper, a, b) for a, b in zip(pieces[0::2], pieces[1::2])]
            got = permute(jnp.concatenate(send, 1), lambda q, x, s: (q, x, s ^ bit))
            width = keep[0].shape[1]
            pieces = [a + got[:, i * width : (i + 1) * width] for i, a in enumerate(keep)]
            bit *= 2
        return pieces[0]

    def spread(fresh, q, x):
        rounds = [permute(fresh, lambda q, x, s, k=k: ((s + k) % n_src, x, q)) for k in range(n_src)]
        turns = [rounds] + [
            [permute(one, lambda q, x, s, i=i: (q, (x + i) % fold, s)) for one in rounds]
            for i in range(1, fold)
        ]
        stacked = jnp.stack([jnp.stack(turn) for turn in turns])
        columns = []
        for a in range(fold):
            for b in range(n_src):
                columns.append(stacked[(x - a) % fold, (q - b) % n_src])
        return jnp.concatenate(columns, 1)

    def shards(kernel, history, driving, load_rate, rate_gain, friction, state_decay):
        lags = kernel.shape[0]
        width = driving.shape[1]
        t, s = lax.axis_index("tgt"), lax.axis_index("src")
        q, x = t // fold, t % fold

        def product(rates, lag_kernels):
            return jnp.einsum("lsc,lec->se", rates, lag_kernels, preferred_element_type=jnp.float32)

        ahead = [product(history[: lags - i], kernel[i:]) for i in range(STEPS)]
        state = jnp.zeros(driving.shape, jnp.float32)
        for section in range(STEPS):
            total = ahead[section]
            pieces = [total[:, i * width : (i + 1) * width] for i in range(n_src)]
            summed = scatter_sum(pieces, s)
            stress = driving + (section + 1) * load_rate[None, :] - summed
            slip_rate = jnp.tanh(rate_gain[None, :] * (stress - friction[None, :] * state)).astype(
                jnp.bfloat16
            )
            state = state_decay[None, :] * state + slip_rate.astype(jnp.float32)
            if section + 1 < STEPS:
                fresh = spread(slip_rate, q, x)
                for later in range(section + 1, STEPS):
                    lag = later - section - 1
                    ahead[later] = ahead[later] + product(fresh[None], kernel[lag : lag + 1])
        return (stress, state, slip_rate)

    return shards


def solution(mesh):
    return jax.shard_map(
        marching(mesh.shape["tgt"], mesh.shape["src"]),
        mesh=mesh,
        in_specs=(
            P(None, "tgt", "src"),
            P(None, None, "src"),
            P(None, ("tgt", "src")),
            P(("tgt", "src")),
            P(("tgt", "src")),
            P(("tgt", "src")),
            P(("tgt", "src")),
        ),
        out_specs=(P(None, ("tgt", "src")), P(None, ("tgt", "src")), P(None, ("tgt", "src"))),
        check_vma=False,
    )
```

```python
import functools

import jax
import jax.numpy as jnp
from jax import lax
from jax.experimental import pallas as pl
from jax.experimental.pallas import tpu as pltpu
from jax.sharding import PartitionSpec as P

STEPS = 6
HEAD = 3
AXES = ("tgt", "src")


def copy_lag(lag, source, target, semaphore):
    copy = pltpu.make_async_copy(source.at[lag], target, semaphore)
    copy.start()
    copy.wait()


def lag_copy(kernel, lag):
    return pl.pallas_call(
        functools.partial(copy_lag, lag),
        in_specs=[pl.BlockSpec(memory_space=pltpu.HBM)],
        out_specs=pl.BlockSpec(memory_space=pltpu.VMEM),
        out_shape=jax.ShapeDtypeStruct(kernel.shape[1:], kernel.dtype),
        scratch_shapes=[pltpu.SemaphoreType.DMA],
        compiler_params=pltpu.CompilerParams(vmem_limit_bytes=36 * 2**20),
    )(kernel)


def lag_sums(rates, lag_kernels, count):
    out = lax.conv_general_dilated(
        rates,
        lag_kernels,
        (1,),
        [(count - 1, lag_kernels.shape[0] - rates.shape[0])],
        dimension_numbers=lax.ConvDimensionNumbers((1, 2, 0), (1, 2, 0), (1, 2, 0)),
        preferred_element_type=jnp.float32,
    )
    return [out[count - 1 - i] for i in range(count)]


def marching(n_tgt, n_src):
    fold = n_tgt // n_src
    places = [(q, x, s) for q in range(n_src) for x in range(fold) for s in range(n_src)]

    def flat(q, x, s):
        return (q * fold + x) * n_src + s

    def permute(value, move):
        pairs = [(flat(*place), flat(*move(*place))) for place in places]
        return lax.ppermute(value, AXES, pairs)

    def scatter_sum(pieces, s, early, late):
        bit = 1
        results = [None, None]
        while len(pieces) > 1:
            upper = (s // bit) % 2 == 1
            keep = [jnp.where(upper, b, a) for a, b in zip(pieces[0::2], pieces[1::2])]
            send = [jnp.where(upper, a, b) for a, b in zip(pieces[0::2], pieces[1::2])]
            send = jnp.concatenate(send, 1)
            here = (1 if len(keep) == 1 else 0) if bit > 1 or len(keep) == 1 else 0
            work = (late if len(keep) == 1 else early) if bit == 1 or len(keep) == 1 else None
            if work:
                send, operands = lax.optimization_barrier((send, work[1]))
            got = permute(send, lambda q, x, s: (q, x, s ^ bit))
            if work:
                result = work[0](operands)
                got, results[here] = lax.optimization_barrier((got, result))
            width = keep[0].shape[1]
            pieces = [a + got[:, i * width : (i + 1) * width] for i, a in enumerate(keep)]
            bit *= 2
        return pieces[0], results[0], results[1]

    def spread(fresh, q, x, work):
        rounds = [permute(fresh, lambda q, x, s, k=k: ((s + k) % n_src, x, q)) for k in range(n_src)]
        done = None
        if work:
            rounds[1], operands = lax.optimization_barrier((rounds[1], work[1]))
        turns = [rounds] + [
            [permute(one, lambda q, x, s, i=i: (q, (x + i) % fold, s)) for one in rounds]
            for i in range(1, fold)
        ]
        if work:
            done = work[0](operands)
            turns[-1], done = lax.optimization_barrier((turns[-1], done))
        stacked = jnp.stack([jnp.stack(turn) for turn in turns])
        columns = []
        for a in range(fold):
            for b in range(n_src):
                columns.append(stacked[(x - a) % fold, (q - b) % n_src])
        return jnp.concatenate(columns, 1), done

    def shards(kernel, history, driving, load_rate, rate_gain, friction, state_decay):
        lags, rows, _ = kernel.shape
        width = driving.shape[1]
        t, s = lax.axis_index("tgt"), lax.axis_index("src")
        q, x = t // fold, t % fold
        parts = 4
        part = rows // parts
        near = {}

        def quarter(i):
            def work(rates):
                return lag_sums(rates, kernel[HEAD:, i * part : (i + 1) * part], STEPS - HEAD)

            return work, history

        def fetch(lag):
            def work(whole):
                return lag_copy(whole, lag)

            return work, kernel

        def add_lag(total, rates, lag):
            return total + jnp.einsum(
                "sc,ec->se", rates, near[lag], preferred_element_type=jnp.float32
            )

        ahead = lag_sums(history, kernel, HEAD)
        slips = []
        quarters = []

        def add(section, lag_list):
            def work(operands):
                total, rates = operands
                for lag, one in zip(lag_list, rates):
                    total = add_lag(total, one, lag)
                return total

            return work, (ahead[section], [slips[section - 1 - lag] for lag in lag_list])

        state = jnp.zeros(driving.shape, jnp.float32)
        for section in range(STEPS):
            total = ahead[section]
            if section:
                total = add_lag(total, slips[-1], 0)
            pieces = [total[:, i * width : (i + 1) * width] for i in range(n_src)]
            last = section + 1 == STEPS
            early = None if last else fetch(section)
            middle = None
            if section < 2:
                middle = quarter(2 * section)
            elif not last:
                middle = add(section + 1, range(1, min(section, 3)))
            summed, got, result = scatter_sum(pieces, s, early, middle)
            if early:
                near[section] = got
            if section < 2:
                quarters.append(result)
            elif not last:
                ahead[section + 1] = result
            stress = driving + (section + 1) * load_rate[None, :] - summed
            slip_rate = jnp.tanh(rate_gain[None, :] * (stress - friction[None, :] * state)).astype(
                jnp.bfloat16
            )
            state = state_decay[None, :] * state + slip_rate.astype(jnp.float32)
            if last:
                break
            if section == 0:
                work = quarter(1)
            elif section == 1:
                rest, sums = quarter(3), add(2, [1])
                work = (lambda o: (rest[0](o[0]), sums[0](o[1]))), (rest[1], sums[1])
            else:
                work = add(section + 1, range(min(section, 3), section + 1))
            fresh, result = spread(slip_rate, q, x, work)
            if section == 0:
                quarters.append(result)
            elif section == 1:
                quarters.append(result[0])
                ahead[2] = result[1]
                ahead += [jnp.concatenate(one, 1) for one in zip(*quarters)]
            else:
                ahead[section + 1] = result
            slips.append(fresh)
        return (stress, state, slip_rate)

    return shards


def solution(mesh):
    return jax.shard_map(
        marching(mesh.shape["tgt"], mesh.shape["src"]),
        mesh=mesh,
        in_specs=(
            P(None, "tgt", "src"),
            P(None, None, "src"),
            P(None, ("tgt", "src")),
            P(("tgt", "src")),
            P(("tgt", "src")),
            P(("tgt", "src")),
            P(("tgt", "src")),
        ),
        out_specs=(P(None, ("tgt", "src")), P(None, ("tgt", "src")), P(None, ("tgt", "src"))),
        check_vma=False,
    )
```

```python
import functools

import jax
import jax.numpy as jnp
from jax import lax
from jax.experimental import pallas as pl
from jax.experimental.pallas import tpu as pltpu
from jax.sharding import PartitionSpec as P

STEPS = 6
HEAD = 4
COPIES = 4
RADIX = 4
AXES = ("tgt", "src")
PLAN = (
    ((("old", 0),), (("old", 1), ("copy", 0))),
    ((("copy", 1),), (("old", 2), ("lag", 1))),
    ((("lag", 1), ("copy", 2)), (("lag", 2), ("old", 3))),
    ((("lag", 1), ("lag", 2)), (("copy", 3), ("lag", 3))),
    ((("lag", 1), ("lag", 2)), (("lag", 3), ("lag", 4))),
)
PARTS = 4


def copy_lag(lag, source, target, semaphore):
    block = target.shape[0] // COPIES
    copies = []
    for i in range(COPIES):
        rows = pl.ds(i * block, block)
        copies.append(
            pltpu.make_async_copy(source.at[lag, rows], target.at[rows], semaphore.at[i])
        )
    for copy in copies:
        copy.start()
    for copy in copies:
        copy.wait()


def lag_copy(kernel, lag):
    return pl.pallas_call(
        functools.partial(copy_lag, lag),
        in_specs=[pl.BlockSpec(memory_space=pltpu.HBM)],
        out_specs=pl.BlockSpec(memory_space=pltpu.VMEM),
        out_shape=jax.ShapeDtypeStruct(kernel.shape[1:], kernel.dtype),
        scratch_shapes=[pltpu.SemaphoreType.DMA((COPIES,))],
        compiler_params=pltpu.CompilerParams(vmem_limit_bytes=36 * 2**20),
    )(kernel)


def lag_sums(rates, lag_kernels, count):
    out = lax.conv_general_dilated(
        rates,
        lag_kernels,
        (1,),
        [(count - 1, lag_kernels.shape[0] - rates.shape[0])],
        dimension_numbers=lax.ConvDimensionNumbers((1, 2, 0), (1, 2, 0), (1, 2, 0)),
        preferred_element_type=jnp.float32,
    )
    return [out[count - 1 - i] for i in range(count)]


def marching(n_tgt, n_src):
    fold = n_tgt // n_src
    places = [(q, x, s) for q in range(n_src) for x in range(fold) for s in range(n_src)]

    def flat(q, x, s):
        return (q * fold + x) * n_src + s

    def permute(value, move):
        pairs = [(flat(*place), flat(*move(*place))) for place in places]
        return lax.ppermute(value, AXES, pairs)

    def scatter_sum(pieces, s, work):
        step, result = 1, None
        while len(pieces) > 1:
            base = min(RADIX, len(pieces))
            digit = (s // step) % base
            groups = [jnp.concatenate(pieces[d::base], 1) for d in range(base)]
            sends = []
            for j in range(base):
                part = lax.select_n(digit, *[groups[d ^ j] for d in range(base)])
                sends.append(part if j * step < 2 else part.astype(jnp.bfloat16))
            last = len(pieces) == base
            if last and work:
                sends, operands = lax.optimization_barrier((sends, work[1]))
            got = [
                permute(sends[j], lambda q, x, s, j=j: (q, x, s ^ (j * step)))
                for j in range(1, base)
            ]
            if last and work:
                got, result = lax.optimization_barrier((got, work[0](operands)))
            total = sends[0]
            for one in got:
                total = total + one.astype(jnp.float32)
            width = pieces[0].shape[1]
            pieces = [total[:, i : i + width] for i in range(0, total.shape[1], width)]
            step *= base
        return pieces[0], result

    def spread(fresh, q, x, work):
        rounds = [permute(fresh, lambda q, x, s, k=k: ((s + k) % n_src, x, q)) for k in range(n_src)]
        result = None
        pairs = [jnp.stack(rounds[k : k + 2]) for k in range(0, n_src, 2)]
        if work:
            pairs[-1], operands = lax.optimization_barrier((pairs[-1], work[1]))
        turns = [pairs] + [
            [permute(one, lambda q, x, s, i=i: (q, (x + i) % fold, s)) for one in pairs]
            for i in range(1, fold)
        ]
        if work:
            turns[-1], result = lax.optimization_barrier((turns[-1], work[0](operands)))
        stacked = jnp.stack([jnp.concatenate(turn) for turn in turns])
        columns = []
        for a in range(fold):
            for b in range(n_src):
                columns.append(stacked[(x - a) % fold, (q - b) % n_src])
        return jnp.concatenate(columns, 1), result

    def shards(kernel, history, driving, load_rate, rate_gain, friction, state_decay):
        _, rows, _ = kernel.shape
        width = driving.shape[1]
        part = rows // PARTS
        t, s = lax.axis_index("tgt"), lax.axis_index("src")
        q, x = t // fold, t % fold
        near, slips, late = {}, [], []
        ahead = lag_sums(history, kernel, HEAD)

        def product(rates, lag):
            operator = near[lag] if lag in near else kernel[lag]
            return jnp.einsum("sc,ec->se", rates, operator, preferred_element_type=jnp.float32)

        def window(section, tasks):
            feeds = []
            for kind, which in tasks:
                feeds.append({"copy": kernel, "old": history}.get(kind))
                if kind == "lag":
                    feeds[-1] = slips[section - which]
            total = [ahead[section + 1]] if any(kind == "lag" for kind, _ in tasks) else []

            def work(operands):
                total, feeds = operands
                made = []
                for (kind, which), feed in zip(tasks, feeds):
                    if kind == "copy":
                        near[which] = lag_copy(feed, which)
                        made.append(near[which])
                    elif kind == "lag":
                        total = [total[0] + product(feed, which)]
                    else:
                        lag_kernels = kernel[HEAD:, which * part : (which + 1) * part]
                        made.append(lag_sums(feed, lag_kernels, STEPS - HEAD))
                return total, made

            return work, (total, feeds)

        def settle(section, tasks, result):
            total, made = result
            if total:
                ahead[section + 1] = total[0]
            made = iter(made)
            for kind, which in tasks:
                if kind == "copy":
                    near[which] = next(made)
                elif kind == "old":
                    late.append(next(made))
                    if len(late) == PARTS:
                        ahead.extend(jnp.concatenate(one, 1) for one in zip(*late))

        state = jnp.zeros(driving.shape, jnp.float32)
        for section in range(STEPS):
            total = ahead[section]
            if section:
                total = total + product(slips[-1], 0)
            pieces = [total[:, i * width : (i + 1) * width] for i in range(n_src)]
            beside_sum, beside_spread = PLAN[section] if section + 1 < STEPS else (None, None)
            summed, result = scatter_sum(pieces, s, beside_sum and window(section, beside_sum))
            if beside_sum:
                settle(section, beside_sum, result)
            stress = driving + (section + 1) * load_rate[None, :] - summed
            slip_rate = jnp.tanh(rate_gain[None, :] * (stress - friction[None, :] * state)).astype(
                jnp.bfloat16
            )
            state = state_decay[None, :] * state + slip_rate.astype(jnp.float32)
            if section + 1 < STEPS:
                fresh, result = spread(slip_rate, q, x, window(section, beside_spread))
                settle(section, beside_spread, result)
                slips.append(fresh)
        return (stress, state, slip_rate)

    return shards


def solution(mesh):
    return jax.shard_map(
        marching(mesh.shape["tgt"], mesh.shape["src"]),
        mesh=mesh,
        in_specs=(
            P(None, "tgt", "src"),
            P(None, None, "src"),
            P(None, ("tgt", "src")),
            P(("tgt", "src")),
            P(("tgt", "src")),
            P(("tgt", "src")),
            P(("tgt", "src")),
        ),
        out_specs=(P(None, ("tgt", "src")), P(None, ("tgt", "src")), P(None, ("tgt", "src"))),
        check_vma=False,
    )
```

```python
import functools

import jax
import jax.numpy as jnp
from jax import lax
from jax.experimental import pallas as pl
from jax.experimental.pallas import tpu as pltpu
from jax.sharding import PartitionSpec as P

STEPS = 6
HEAD = 4
RADIX = 4
AXES = ("tgt", "src")
PLAN = (
    ((("old", 0),), (("copy", 0), ("own", 0), ("old", 1))),
    ((("copy", 1), ("lag", 1)), (("own", 0), ("old", 2))),
    ((("lag", 1), ("copy", 2)), (("own", 0), ("lag", 2), ("old", 3))),
    ((("lag", 1), ("copy", 3)), (("own", 0), ("lag", 2), ("lag", 3))),
    ((("lag", 1), ("copy", 4)), (("own", 0), ("lag", 2), ("lag", 3), ("lag", 4))),
)
PARTS = 4


def copy_columns(lag, starts, width, source, target, semaphore):
    copies = []
    for i, start in enumerate(starts()):
        copies.append(
            pltpu.make_async_copy(
                source.at[lag, :, pl.ds(pl.multiple_of(start, width), width)],
                target.at[:, pl.ds(i * width, width)],
                semaphore.at[i],
            )
        )
    for copy in copies:
        copy.start()
    for copy in copies:
        copy.wait()


def lag_copy(kernel, lag, starts, width):
    count = len(starts())
    if width % 128:
        columns = [lax.dynamic_slice_in_dim(kernel[lag], start, width, 1) for start in starts()]
        return jnp.concatenate(columns, 1)
    return pl.pallas_call(
        functools.partial(copy_columns, lag, starts, width),
        in_specs=[pl.BlockSpec(memory_space=pltpu.HBM)],
        out_specs=pl.BlockSpec(memory_space=pltpu.VMEM),
        out_shape=jax.ShapeDtypeStruct((kernel.shape[1], count * width), kernel.dtype),
        scratch_shapes=[pltpu.SemaphoreType.DMA((count,))],
        compiler_params=pltpu.CompilerParams(vmem_limit_bytes=36 * 2**20),
    )(kernel)


def lag_sums(rates, lag_kernels, count):
    out = lax.conv_general_dilated(
        rates,
        lag_kernels,
        (1,),
        [(count - 1, lag_kernels.shape[0] - rates.shape[0])],
        dimension_numbers=lax.ConvDimensionNumbers((1, 2, 0), (1, 2, 0), (1, 2, 0)),
        preferred_element_type=jnp.float32,
    )
    return [out[count - 1 - i] for i in range(count)]


def marching(n_tgt, n_src):
    fold = n_tgt // n_src
    order = [0] + list(range(n_src - 1, 0, -1))
    places = [(q, x, s) for q in range(n_src) for x in range(fold) for s in range(n_src)]

    def flat(q, x, s):
        return (q * fold + x) * n_src + s

    def permute(value, move):
        pairs = [(flat(*place), flat(*move(*place))) for place in places]
        return lax.ppermute(value, AXES, pairs)

    def scatter_sum(pieces, s, work):
        step, result = 1, None
        while len(pieces) > 1:
            base = min(RADIX, len(pieces))
            digit = (s // step) % base
            groups = [jnp.concatenate(pieces[d::base], 1) for d in range(base)]
            sends = []
            for j in range(base):
                part = lax.select_n(digit, *[groups[d ^ j] for d in range(base)])
                sends.append(part if j * step < 2 else part.astype(jnp.bfloat16))
            last = len(pieces) == base
            if last and work:
                sends, operands = lax.optimization_barrier((sends, work[1]))
            got = [
                permute(sends[j], lambda q, x, s, j=j: (q, x, s ^ (j * step)))
                for j in range(1, base)
            ]
            if last and work:
                got, result = lax.optimization_barrier((got, work[0](operands)))
            total = sends[0]
            for one in got:
                total = total + one.astype(jnp.float32)
            width = pieces[0].shape[1]
            pieces = [total[:, i : i + width] for i in range(0, total.shape[1], width)]
            step *= base
        return pieces[0], result

    def spread(fresh, work):
        rounds = [permute(fresh, lambda q, x, s, k=k: ((s + k) % n_src, x, q)) for k in order]
        pairs = [jnp.stack(rounds[k : k + 2]) for k in range(0, n_src, 2)]
        pairs[-1], operands = lax.optimization_barrier((pairs[-1], work[1]))

        def columns(turn):
            return jnp.concatenate([one for pair in turn for one in pair], 1)

        turns = [
            [permute(one, lambda q, x, s, i=i: (q, (x + i) % fold, s)) for one in pairs]
            for i in range(1, fold)
        ]
        own = columns(pairs)
        turns, result = lax.optimization_barrier((turns, work[0](operands, own)))
        return [own] + [columns(turn) for turn in turns], result

    def shards(kernel, history, driving, load_rate, rate_gain, friction, state_decay):
        _, rows, _ = kernel.shape
        width = driving.shape[1]
        part_rows = rows // PARTS
        s = lax.axis_index("src")
        near, slips, late = {}, [], []
        ahead = lag_sums(history, kernel, HEAD)

        def starts(turns):
            t = lax.axis_index("tgt")
            q, x = t // fold, t % fold
            return [
                (((x - i + fold) % fold) * n_src + (q - k + n_src) % n_src) * width
                for i in turns
                for k in order
            ]

        def product(rates, operator):
            return jnp.einsum("sc,ec->se", rates, operator, preferred_element_type=jnp.float32)

        def window(section, tasks):
            feeds = []
            for kind, which in tasks:
                feeds.append({"copy": kernel, "old": history}.get(kind, ()))
                if kind == "lag":
                    feeds[-1] = jnp.concatenate(slips[section - which], 1)
            sums = any(kind in ("lag", "own") for kind, _ in tasks)

            def work(operands, own=None):
                total, feeds = operands
                made = []
                for (kind, which), feed in zip(tasks, feeds):
                    if kind == "copy":
                        parts = [range(fold)] if which else [range(1), range(1, fold)]
                        near[which] = [
                            lag_copy(feed, which, functools.partial(starts, part), width)
                            for part in parts
                            if len(part)
                        ]
                        made.append(near[which])
                    elif kind == "lag":
                        total = [total[0] + product(feed, near[which][0])]
                    elif kind == "own":
                        total = [total[0] + product(own, near[0][0])]
                    else:
                        lag_kernels = kernel[HEAD:, which * part_rows : (which + 1) * part_rows]
                        made.append(lag_sums(feed, lag_kernels, STEPS - HEAD))
                return total, made

            return work, ([ahead[section + 1]] if sums else [], feeds)

        def settle(section, tasks, result):
            total, made = result
            if total:
                ahead[section + 1] = total[0]
            made = iter(made)
            for kind, which in tasks:
                if kind == "copy":
                    near[which] = next(made)
                elif kind == "old":
                    late.append(next(made))
                    if len(late) == PARTS:
                        ahead.extend(jnp.concatenate(one, 1) for one in zip(*late))

        state = jnp.zeros(driving.shape, jnp.float32)
        for section in range(STEPS):
            total = ahead[section]
            if section and fold > 1:
                total = total + product(jnp.concatenate(slips[-1][1:], 1), near[0][1])
            pieces = [total[:, i * width : (i + 1) * width] for i in range(n_src)]
            beside_sum, beside_spread = PLAN[section] if section + 1 < STEPS else (None, None)
            summed, result = scatter_sum(pieces, s, beside_sum and window(section, beside_sum))
            if beside_sum:
                settle(section, beside_sum, result)
            stress = driving + (section + 1) * load_rate[None, :] - summed
            slip_rate = jnp.tanh(rate_gain[None, :] * (stress - friction[None, :] * state)).astype(
                jnp.bfloat16
            )
            state = state_decay[None, :] * state + slip_rate.astype(jnp.float32)
            if section + 1 < STEPS:
                fresh, result = spread(slip_rate, window(section, beside_spread))
                settle(section, beside_spread, result)
                slips.append(fresh)
        return (stress, state, slip_rate)

    return shards


def solution(mesh):
    return jax.shard_map(
        marching(mesh.shape["tgt"], mesh.shape["src"]),
        mesh=mesh,
        in_specs=(
            P(None, "tgt", "src"),
            P(None, None, "src"),
            P(None, ("tgt", "src")),
            P(("tgt", "src")),
            P(("tgt", "src")),
            P(("tgt", "src")),
            P(("tgt", "src")),
        ),
        out_specs=(P(None, ("tgt", "src")), P(None, ("tgt", "src")), P(None, ("tgt", "src"))),
        check_vma=False,
    )
```

```python
import functools

import jax
import jax.numpy as jnp
from jax import lax
from jax.experimental import pallas as pl
from jax.experimental.pallas import tpu as pltpu
from jax.sharding import PartitionSpec as P

STEPS = 6
HEAD = 4
RADIX = 2
AXES = ("tgt", "src")
PLAN = (
    ((("old", 0),), (("copy", 0), ("own", 0), ("old", 1))),
    ((("copy", 1), ("lag", 1)), (("own", 0), ("old", 2))),
    ((("lag", 1), ("copy", 2)), (("own", 0), ("lag", 2), ("old", 3))),
    ((("lag", 1), ("copy", 3)), (("own", 0), ("lag", 2), ("lag", 3))),
    ((("lag", 1), ("copy", 4)), (("own", 0), ("lag", 2), ("lag", 3), ("lag", 4))),
)
PARTS = 4


def copy_columns(lag, starts, width, source, target, semaphore):
    copies = []
    for i, start in enumerate(starts()):
        copies.append(
            pltpu.make_async_copy(
                source.at[lag, :, pl.ds(pl.multiple_of(start, width), width)],
                target.at[:, pl.ds(i * width, width)],
                semaphore.at[i],
            )
        )
    for copy in copies:
        copy.start()
    for copy in copies:
        copy.wait()


def lag_copy(kernel, lag, starts, width):
    count = len(starts())
    if width % 128:
        columns = [lax.dynamic_slice_in_dim(kernel[lag], start, width, 1) for start in starts()]
        return jnp.concatenate(columns, 1)
    return pl.pallas_call(
        functools.partial(copy_columns, lag, starts, width),
        in_specs=[pl.BlockSpec(memory_space=pltpu.HBM)],
        out_specs=pl.BlockSpec(memory_space=pltpu.VMEM),
        out_shape=jax.ShapeDtypeStruct((kernel.shape[1], count * width), kernel.dtype),
        scratch_shapes=[pltpu.SemaphoreType.DMA((count,))],
        compiler_params=pltpu.CompilerParams(vmem_limit_bytes=36 * 2**20),
    )(kernel)


def lag_sums(rates, lag_kernels, count):
    out = lax.conv_general_dilated(
        rates,
        lag_kernels,
        (1,),
        [(count - 1, lag_kernels.shape[0] - rates.shape[0])],
        dimension_numbers=lax.ConvDimensionNumbers((1, 2, 0), (1, 2, 0), (1, 2, 0)),
        preferred_element_type=jnp.float32,
    )
    return [out[count - 1 - i] for i in range(count)]


def marching(n_tgt, n_src):
    fold = n_tgt // n_src
    order = [0] + list(range(n_src - 1, 0, -1))
    places = [(q, x, s) for q in range(n_src) for x in range(fold) for s in range(n_src)]

    def flat(q, x, s):
        return (q * fold + x) * n_src + s

    def permute(value, move):
        pairs = [(flat(*place), flat(*move(*place))) for place in places]
        return lax.ppermute(value, AXES, pairs)

    def scatter_sum(pieces, s, work):
        step, result = 1, None
        while len(pieces) > 1:
            base = min(RADIX, len(pieces))
            digit = (s // step) % base
            groups = [jnp.concatenate(pieces[d::base], 1) for d in range(base)]
            sends = []
            for j in range(base):
                part = lax.select_n(digit, *[groups[d ^ j] for d in range(base)])
                sends.append(part)
            last = len(pieces) == base
            if last and work:
                sends, operands = lax.optimization_barrier((sends, work[1]))
            got = [
                permute(sends[j], lambda q, x, s, j=j: (q, x, s ^ (j * step)))
                for j in range(1, base)
            ]
            if last and work:
                got, result = lax.optimization_barrier((got, work[0](operands)))
            total = sends[0]
            for one in got:
                total = total + one.astype(jnp.float32)
            width = pieces[0].shape[1]
            pieces = [total[:, i : i + width] for i in range(0, total.shape[1], width)]
            step *= base
        return pieces[0], result

    def spread(fresh, work):
        rounds = [permute(fresh, lambda q, x, s, k=k: ((s + k) % n_src, x, q)) for k in order]
        pairs = [jnp.stack(rounds[k : k + 2]) for k in range(0, n_src, 2)]
        pairs[-1], operands = lax.optimization_barrier((pairs[-1], work[1]))

        def columns(turn):
            return jnp.concatenate([one for pair in turn for one in pair], 1)

        turns = [
            [permute(one, lambda q, x, s, i=i: (q, (x + i) % fold, s)) for one in pairs]
            for i in range(1, fold)
        ]
        own = columns(pairs)
        turns, result = lax.optimization_barrier((turns, work[0](operands, own)))
        return [own] + [columns(turn) for turn in turns], result

    def shards(kernel, history, driving, load_rate, rate_gain, friction, state_decay):
        _, rows, _ = kernel.shape
        width = driving.shape[1]
        part_rows = rows // PARTS
        s = lax.axis_index("src")
        near, slips, late = {}, [], []
        ahead = lag_sums(history, kernel, HEAD)

        def starts(turns):
            t = lax.axis_index("tgt")
            q, x = t // fold, t % fold
            return [
                (((x - i + fold) % fold) * n_src + (q - k + n_src) % n_src) * width
                for i in turns
                for k in order
            ]

        def product(rates, operator):
            return jnp.einsum("sc,ec->se", rates, operator, preferred_element_type=jnp.float32)

        def window(section, tasks):
            feeds = []
            for kind, which in tasks:
                feeds.append({"copy": kernel, "old": history}.get(kind, ()))
                if kind == "lag":
                    feeds[-1] = jnp.concatenate(slips[section - which], 1)
            sums = any(kind in ("lag", "own") for kind, _ in tasks)

            def work(operands, own=None):
                total, feeds = operands
                made = []
                for (kind, which), feed in zip(tasks, feeds):
                    if kind == "copy":
                        parts = [range(fold)] if which else [range(1), range(1, fold)]
                        near[which] = [
                            lag_copy(feed, which, functools.partial(starts, part), width)
                            for part in parts
                            if len(part)
                        ]
                        made.append(near[which])
                    elif kind == "lag":
                        total = [total[0] + product(feed, near[which][0])]
                    elif kind == "own":
                        total = [total[0] + product(own, near[0][0])]
                    else:
                        lag_kernels = kernel[HEAD:, which * part_rows : (which + 1) * part_rows]
                        made.append(lag_sums(feed, lag_kernels, STEPS - HEAD))
                return total, made

            return work, ([ahead[section + 1]] if sums else [], feeds)

        def settle(section, tasks, result):
            total, made = result
            if total:
                ahead[section + 1] = total[0]
            made = iter(made)
            for kind, which in tasks:
                if kind == "copy":
                    near[which] = next(made)
                elif kind == "old":
                    late.append(next(made))
                    if len(late) == PARTS:
                        ahead.extend(jnp.concatenate(one, 1) for one in zip(*late))

        state = jnp.zeros(driving.shape, jnp.float32)
        for section in range(STEPS):
            total = ahead[section]
            if section and fold > 1:
                total = total + product(jnp.concatenate(slips[-1][1:], 1), near[0][1])
            pieces = [total[:, i * width : (i + 1) * width] for i in range(n_src)]
            beside_sum, beside_spread = PLAN[section] if section + 1 < STEPS else (None, None)
            summed, result = scatter_sum(pieces, s, beside_sum and window(section, beside_sum))
            if beside_sum:
                settle(section, beside_sum, result)
            stress = driving + (section + 1) * load_rate[None, :] - summed
            slip_rate = jnp.tanh(rate_gain[None, :] * (stress - friction[None, :] * state)).astype(
                jnp.bfloat16
            )
            state = state_decay[None, :] * state + slip_rate.astype(jnp.float32)
            if section + 1 < STEPS:
                fresh, result = spread(slip_rate, window(section, beside_spread))
                settle(section, beside_spread, result)
                slips.append(fresh)
        return (stress, state, slip_rate)

    return shards


def solution(mesh):
    return jax.shard_map(
        marching(mesh.shape["tgt"], mesh.shape["src"]),
        mesh=mesh,
        in_specs=(
            P(None, "tgt", "src"),
            P(None, None, "src"),
            P(None, ("tgt", "src")),
            P(("tgt", "src")),
            P(("tgt", "src")),
            P(("tgt", "src")),
            P(("tgt", "src")),
        ),
        out_specs=(P(None, ("tgt", "src")), P(None, ("tgt", "src")), P(None, ("tgt", "src"))),
        check_vma=False,
    )
```
